256 devices in a mesh: snode: 32 (over y, z), col: 8 (over x, core).
Axes of the slice: x: 4, y: 4, z: 8, core: 2. Of those that a mesh axis runs over, the one named last changes fastest.
Arguments:
- parent_sigma: float32 [32, 128, 32, 128], P('snode', 'col'), may hold values from -6 to 6
- owner: int32 [32], replicated, may hold values from 0 to 31, each once
- ancestors: int32 [32, 16], P('snode'), may hold values from 0 to 31, all different within a row
- lfactors: bfloat16 [49152, 1536], P('snode'), may hold values from -3 to 3, as said below
- panels: bfloat16 [65536, 1536], P('snode', 'col'), may hold values from -0.01953125 to 0.01953125
Outputs:
- sigma_anc: float32 [32, 16, 128, 1536], P('snode', None, 'col')
- sigma_diag: float32 [49152, 1536], P('snode', 'col')
The draws below stay inside these ranges and needn't reach their ends.
Inputs may be any that keep to these rules, and one draw needn't show every extreme that they name: `ancestors`: each row names 16 different parent tiles, and every parent tile is named by some supernode. `owner`: A permutation of the parent tiles. `lfactors`: each 1536 x 1536 block is lower triangular with diagonal entries between 1.5 and 3.
All inputs are finite; a program needn't handle non-finite values.
Results may differ from the reference program's by a relative error of at most 0.0003.
Values may be sent and summed in bfloat16 or wider, within the bound.
No kernel may reach another device: no remote copies, remote signals or barrier semaphores. Data moves between devices by JAX's collectives and lax.ppermute only.
A program may use at most 128 MiB of HBM per device.

```python
import math
import jax
import jax.numpy as jnp
from jax import lax

NS = 1536
TILE = 128
ANC_T = 16
PTILES = 32
SNODES = 32
ANC = 2048


def draw_lfactors(key, part):
    key_diag, key_off = jax.random.split(key)
    diagonal = jnp.exp(jax.random.uniform(key_diag, (SNODES * NS, 1), jnp.float32, math.log(1.5), math.log(3.0)))
    spread = 2.6 / math.sqrt(NS)
    lower_part = jnp.clip(jax.random.normal(key_off, (SNODES * NS, NS), jnp.float32), -4.0, 4.0) * spread
    row_ids = jnp.arange(SNODES * NS)[:, None] % NS
    col_ids = jnp.arange(NS)[None, :]
    values = jnp.where(col_ids < row_ids, lower_part, jnp.where(col_ids == row_ids, diagonal, 0.0))
    return values.astype(jnp.bfloat16)


def shard_levels(own_key, shape, shards, smallest, largest):
    loudness, own = 1.0, jax.random.fold_in(own_key, 6)
    for axis_at, blocks in shards:
        draws = jnp.exp(jax.random.uniform(jax.random.fold_in(own, axis_at), (blocks,), jnp.float32, smallest / len(shards), largest / len(shards)))
        loudness = loudness * jnp.repeat(draws, shape[axis_at] // blocks).reshape([-1 if axis == axis_at else 1 for axis in range(len(shape))])
    return loudness


def different_ones(own_key, rows, number_of, top, lift):
    ranking = jax.random.permutation(jax.random.fold_in(own_key, 1), number_of)
    boost = ranking
    for power in range(3):
        boost = boost * boost // number_of
    boost = boost * lift // number_of
    tickets = jax.random.randint(jax.random.fold_in(own_key, 2), (rows, number_of), 0, 4096) + boost
    holders = jax.random.permutation(jax.random.fold_in(own_key, 3), rows)[jnp.arange(number_of) % rows]
    tickets = jnp.where(jnp.arange(rows)[:, None] == holders[None, :], 1 << 14, tickets)
    merit = tickets * number_of + jnp.arange(number_of)
    return lax.top_k(merit.astype(jnp.int32), top)[1].astype(jnp.int32)


def noise(key, dims, scale, most, cuts=(), held_as=jnp.bfloat16):
    array = jax.random.normal(key, dims, jnp.float32) * scale
    if len(cuts) > 0:
        array = shard_levels(key, dims, cuts, -0.22, 0.18) * array
    return jnp.clip(array, min=-most, max=most).astype(held_as)


def setup_inputs(seed: int = 0) -> dict:
    key_of = jax.random.split(jax.random.key(seed), 6)
    parent_sigma = noise(key_of[0], (PTILES, TILE, PTILES, TILE), 1.0, 6.0, ((0, 32), (1, 8)), jnp.float32)
    owner = jax.random.permutation(key_of[1], PTILES).astype(jnp.int32)
    ancestors = different_ones(key_of[2], SNODES, PTILES, ANC_T, 8192)
    lfactors = draw_lfactors(jax.random.fold_in(key_of[5], 71), 0)
    panels = noise(key_of[4], (SNODES * ANC, NS), (ANC * (NS // 48 + 8)) ** -0.5, 0.01953125, ((0, 32), (1, 8)))
    return {"parent_sigma": parent_sigma, "owner": owner, "ancestors": ancestors, "lfactors": lfactors, "panels": panels}


def reference(parent_sigma, owner, ancestors, lfactors, panels):
    identity = jnp.eye(NS, dtype=jnp.float32)

    def per_node(packed):
        anc_row, factor, panel_rows = packed
        slot_ids = owner[anc_row]
        row_tiles = jnp.take(parent_sigma, slot_ids, axis=0)
        sub_sigma = jnp.take(row_tiles, anc_row, axis=2).reshape(ANC, ANC)
        factor_f = factor.astype(jnp.float32)
        half_inv = lax.linalg.triangular_solve(factor_f, identity, left_side=True, lower=True)
        diag_inv = lax.linalg.triangular_solve(factor_f, half_inv, left_side=True, lower=True, transpose_a=True)
        panel_wide = panel_rows.astype(jnp.float32)
        anc_sig = -jnp.dot(sub_sigma, panel_wide, precision=lax.Precision.HIGHEST)
        diag_sig = diag_inv - jnp.dot(panel_wide.T, anc_sig, precision=lax.Precision.HIGHEST)
        return (anc_sig.reshape(ANC_T, TILE, NS), diag_sig)
    anc_all, diag_all = lax.map(per_node, (ancestors, lfactors.reshape(SNODES, NS, NS), panels.reshape(SNODES, ANC, NS)))
    return (anc_all, diag_all.reshape(SNODES * NS, NS))
```

```python
import functools
import jax
import jax.numpy as jnp
from jax import lax
from jax.experimental import pallas as pl
from jax.experimental.pallas import tpu as pltpu
from jax.sharding import Mesh, PartitionSpec as P


F32, BF16, I16 = jnp.float32, jnp.bfloat16, jnp.int16
T = 128
TOP = 32767.0
NT = (((1,), (1,)), ((), ()))
NN = (((1,), (0,)), ((), ()))
TN = (((0,), (1,)), ((), ()))


def dot(a, b, dims=NN):
    return lax.dot_general(a, b, dims, preferred_element_type=F32)


def split(v):
    hi = v.astype(BF16)
    return hi, (v - hi.astype(F32)).astype(BF16)


def dot3(a, b, dims=NN):
    ah, al = a
    bh, bl = b
    return dot(ah, bh, dims) + (dot(ah, bl, dims) + dot(al, bh, dims))


def code_of(top):
    return jnp.clip(jnp.ceil(jnp.log2(top) * 256.0), -32000.0, 32000.0)


def scale_of(code):
    return jnp.exp2(code * (1.0 / 256.0))


def encode(v, code):
    q = jnp.round(v * (TOP / scale_of(code)))
    return jnp.clip(q, -TOP, TOP).astype(jnp.int32).astype(I16)


def widen(q):
    return q.astype(jnp.int32).astype(F32)


def code_rows_kernel(x_ref, a_ref, b_ref):
    rows, tiles = x_ref.shape[0], x_ref.shape[1]
    half = rows // 2
    lane = lax.broadcasted_iota(jnp.int32, (rows, T), 1)
    acc = jnp.zeros((rows, T), F32)
    for t in range(tiles):
        v = x_ref[:, t, :]
        code = code_of(jnp.max(jnp.abs(v), axis=1, keepdims=True))
        q = encode(v, code)
        a_ref[t] = q[:half]
        b_ref[t] = q[half:]
        acc = jnp.where(lane == t, code, acc)
    q = acc.astype(jnp.int32).astype(I16)
    a_ref[tiles] = q[:half]
    b_ref[tiles] = q[half:]


def code_rows(x):
    rows, tiles, _ = x.shape
    shape = jax.ShapeDtypeStruct((tiles + 1, rows // 2, T), I16)
    return pl.pallas_call(code_rows_kernel, out_shape=(shape, shape), name="code_rows")(x)


def pick_kernel(lists_ref, x_ref, o_ref):
    dests, picks = o_ref.shape[0], o_ref.shape[2] - 1
    tiles = x_ref.shape[1] - 1
    for d in range(dests):
        for j in range(picks):
            o_ref[d, :, j] = x_ref[:, lists_ref[d, j]]
        o_ref[d, :, picks] = x_ref[:, tiles]


def pick(lists, x):
    dests, picks = lists.shape
    n, _, rows, _ = x.shape
    return pl.pallas_call(
        pick_kernel,
        out_shape=jax.ShapeDtypeStruct((dests, n, picks + 1, rows, T), I16),
        in_specs=[pl.BlockSpec(memory_space=pltpu.SMEM), pl.BlockSpec(memory_space=pltpu.VMEM)],
        out_specs=pl.BlockSpec(memory_space=pltpu.VMEM),
        name="pick",
    )(lists, x)


BLK = 256


def invert_kernel(l_ref, hi_ref, lo_ref):
    n = l_ref.shape[0] // BLK
    row = lax.broadcasted_iota(jnp.int32, (BLK, BLK), 0)
    col = lax.broadcasted_iota(jnp.int32, (BLK, BLK), 1)
    eye = row == col
    blocks, invs = [], []
    for k in range(n):
        b = l_ref[k * BLK:(k + 1) * BLK, k * BLK:(k + 1) * BLK]
        f = b.astype(F32)
        d = jnp.where(eye, f, 0.0)
        rd = 1.0 / jnp.sum(d, axis=1, keepdims=True)
        cd = 1.0 / jnp.sum(d, axis=0, keepdims=True)
        pair = ((row >> 1) == (col >> 1)) & (row > col)
        invs.append(jnp.where(eye, rd, 0.0) - jnp.where(pair, f * rd * cd, 0.0))
        blocks.append(b)
    h = 2
    while h < BLK:
        mask = (row // (2 * h) == col // (2 * h)) & ((row // h) % 2 == 1) & ((col // h) % 2 == 0)
        for k in range(n):
            c = jnp.where(mask, blocks[k].astype(F32), 0.0).astype(BF16)
            ih, il = split(invs[k])
            t = split(dot(c, ih) + dot(c, il))
            invs[k] = invs[k] - dot3((ih, il), t)
        h *= 2
    for k in range(n):
        hi, lo = split(invs[k])
        hi_ref[k] = hi
        lo_ref[k] = lo


def invert(lf):
    n = lf.shape[0] // BLK
    shape = jax.ShapeDtypeStruct((n, BLK, BLK), BF16)
    return pl.pallas_call(invert_kernel, out_shape=(shape, shape), name="invert")(lf)


def forward_kernel(at_ref, l_ref, dh_ref, dl_ref, x_ref, xh, xl):
    m = x_ref.shape[0]
    n = l_ref.shape[0] // BLK
    base = at_ref[0] * m
    row = lax.broadcasted_iota(jnp.int32, (m, BLK), 0) + base
    col = lax.broadcasted_iota(jnp.int32, (m, BLK), 1)
    for k in range(n):
        s = slice(k * BLK, (k + 1) * BLK)
        r = jnp.where(row == col + k * BLK, 1.0, 0.0)
        if k:
            lk = l_ref[s, :k * BLK]
            r = r - (dot(xh[:, :k * BLK], lk, NT) + dot(xl[:, :k * BLK], lk, NT))
        v = dot3(split(r), (dh_ref[k], dl_ref[k]), NT)
        x_ref[:, s] = v
        xh[:, s], xl[:, s] = split(v)


def forward(at, lf, dh, dl, m):
    order = lf.shape[0]
    vm = pl.BlockSpec(memory_space=pltpu.VMEM)
    return pl.pallas_call(
        forward_kernel,
        out_shape=jax.ShapeDtypeStruct((m, order), F32),
        in_specs=[pl.BlockSpec(memory_space=pltpu.SMEM), vm, vm, vm],
        out_specs=vm,
        scratch_shapes=[pltpu.VMEM((m, order), BF16), pltpu.VMEM((m, order), BF16)],
        name="forward",
    )(at, lf, dh, dl)


def backward_kernel(x_ref, l_ref, dh_ref, dl_ref, y_ref, yh, yl):
    n = l_ref.shape[0] // BLK
    for k in reversed(range(n)):
        s = slice(k * BLK, (k + 1) * BLK)
        r = x_ref[:, s]
        if k < n - 1:
            e = (k + 1) * BLK
            lk = l_ref[e:, s]
            r = r - (dot(yh[:, e:], lk) + dot(yl[:, e:], lk))
        v = dot3(split(r), (dh_ref[k], dl_ref[k]))
        y_ref[:, s] = v
        yh[:, s], yl[:, s] = split(v)


def backward(x, lf, dh, dl):
    m, order = x.shape
    vm = pl.BlockSpec(memory_space=pltpu.VMEM)
    return pl.pallas_call(
        backward_kernel,
        out_shape=jax.ShapeDtypeStruct((m, order), F32),
        in_specs=[vm] * 4,
        out_specs=vm,
        scratch_shapes=[pltpu.VMEM((m, order), BF16), pltpu.VMEM((m, order), BF16)],
        name="backward",
    )(x, lf, dh, dl)


def anc_kernel(slots_ref, anc_ref, pos_ref, a_ref, b_ref, *refs):
    (p0, p1, p2, p3, p4, q0, q1, q2, q3, q4, o_ref, e_ref, w_ref, pt, sh, sl, sc, sem) = refs
    k_all = pt.shape[1]
    m = p0.shape[0]
    h = m // 2
    x, core = pos_ref[0], pos_ref[1]
    copies = []

    def put(src, at, off, n):
        copies.append(pltpu.make_async_copy(src, pt.at[pl.ds(pl.multiple_of(at * m + off, 32), n)], sem.at[len(copies)]))
        copies[-1].start()

    for which, (s0, s1, s2, s3, s4) in enumerate(((p0, p1, p2, p3, p4), (q0, q1, q2, q3, q4))):
        c = core if which == 0 else 1 - core
        put(s0, 2 * x + c, 0, m)
        put(s1, 2 * ((x + 3) % 4) + c, 0, m)
        put(s2, 2 * ((x + 1) % 4) + c, 0, m)
        put(s3, 2 * ((x + 2) % 4) + c, 0, h)
        put(s4, 2 * ((x + 2) % 4) + c, h, h)

    n_anc = o_ref.shape[0] // 16
    rows = 16
    tid = lax.broadcasted_iota(jnp.int32, (T, T), 0)
    for i in range(n_anc):
        s = slots_ref[i]
        ca = widen(a_ref[s // 8, s % 8, n_anc])
        cb = widen(b_ref[s % 8, s // 8, n_anc])
        sc[i * rows:(i + 1) * rows] = scale_of(jnp.concatenate([ca, cb], 0)) * (1.0 / TOP)
    sch, scl = split(sc[...])
    for j in range(n_anc):
        one = jnp.where(tid == anc_ref[j], 1.0, 0.0).astype(BF16)
        wide = dot(sch, one) + dot(scl, one)
        for i in range(n_anc):
            s = slots_ref[i]
            q = jnp.concatenate([widen(a_ref[s // 8, s % 8, j]), widen(b_ref[s % 8, s // 8, j])], 0)
            hi, lo = split(-q * wide[i * rows:(i + 1) * rows])
            sh[i * rows:(i + 1) * rows, j * T:(j + 1) * T] = hi
            sl[i * rows:(i + 1) * rows, j * T:(j + 1) * T] = lo
    for c in copies:
        c.wait()
    out = pltpu.make_async_copy(pt, w_ref, sem.at[len(copies)])
    out.start()
    all_rows = n_anc * rows
    lane = lax.broadcasted_iota(jnp.int32, (all_rows, T), 1)
    sub = lax.broadcasted_iota(jnp.int32, (all_rows, T), 0) % rows
    low = lane < 64
    for g in range(4):
        ps = pt[g * 2 * m:(g + 1) * 2 * m, :]
        v = dot(sh[...], ps, NT) + dot(sl[...], ps, NT)
        o_ref[:, g * 2 * m:(g + 1) * 2 * m] = v
        mid = v[:, T:2 * T]
        for side in range(2):
            whole = v[:, :T] if side == 0 else v[:, 2 * T:]
            keep = low if side == 0 else ~low
            top = jnp.maximum(jnp.abs(whole), jnp.where(keep, jnp.abs(mid), 0.0))
            code = code_of(jnp.max(top, axis=1, keepdims=True))
            e = e_ref.at[2 * g + side]
            e[:all_rows] = encode(whole, code)
            qm = encode(jnp.where(keep, mid, 0.0), code).astype(jnp.int32)
            lo_part = slice(0, 64) if side == 0 else slice(64, 128)
            qh = jnp.concatenate([qm[:all_rows // 2, lo_part], qm[all_rows // 2:, lo_part]], axis=1)
            e[all_rows:all_rows + all_rows // 2] = qh.astype(I16)
            grid = jnp.where(lane == sub, code, 0.0)
            tile = jnp.sum(grid.reshape(n_anc, rows, T), axis=1)
            e[all_rows + all_rows // 2:] = tile.astype(jnp.int32).astype(I16)
    out.wait()


def sigma_anc(slots, anc, pos, a2, b2, blocks):
    n_anc = anc.shape[0]
    m, k_all = blocks[0].shape
    smem = pl.BlockSpec(memory_space=pltpu.SMEM)
    vm = pl.BlockSpec(memory_space=pltpu.VMEM)
    hbm = pl.BlockSpec(memory_space=pl.ANY)
    rows = n_anc * 16
    return pl.pallas_call(
        anc_kernel,
        out_shape=(
            jax.ShapeDtypeStruct((rows, 8 * m), F32),
            jax.ShapeDtypeStruct((8, rows + rows // 2 + n_anc, T), I16),
            jax.ShapeDtypeStruct((8 * m, k_all), BF16),
        ),
        in_specs=[smem, smem, smem, vm, vm] + [hbm] * 10,
        out_specs=(vm, vm, hbm),
        scratch_shapes=[
            pltpu.VMEM((8 * m, k_all), BF16),
            pltpu.VMEM((rows, k_all), BF16),
            pltpu.VMEM((rows, k_all), BF16),
            pltpu.VMEM((rows, T), F32),
            pltpu.SemaphoreType.DMA((11,)),
        ],
        name="sigma_anc",
    )(slots, anc, pos, a2, b2, *blocks)


def diag_kernel(pos_ref, e_ref, y_ref, w_ref, o_ref, ah, al, gh, gl):
    n_anc, rows = 16, 16
    all_rows = n_anc * rows
    lane = lax.broadcasted_iota(jnp.int32, (rows, T), 1)
    sub = lax.broadcasted_iota(jnp.int32, (rows, T), 0)
    for c in range(8):
        e = e_ref.at[c]
        sc = scale_of(widen(e[all_rows + all_rows // 2:])) * (1.0 / TOP)
        cols = []
        for i in range(n_anc):
            cols.append(jnp.sum(jnp.where(lane == sub, sc[i:i + 1], 0.0), axis=1, keepdims=True))
        for i in range(n_anc):
            hi, lo = split(widen(e[i * rows:(i + 1) * rows]) * cols[i])
            at = i * T + c * rows
            ah[at:at + rows] = hi
            al[at:at + rows] = lo
        for i in range(n_anc // 2):
            s = jnp.where(lane < 64, cols[i], cols[i + n_anc // 2])
            hi, lo = split(widen(e[all_rows + i * rows:all_rows + (i + 1) * rows]) * s)
            at = i * T + c * rows
            gh[at:at + rows] = hi
            gl[at:at + rows] = lo
    core = pos_ref[1]
    k_half = gh.shape[0]
    w = w_ref[...]
    v = dot(ah[...], w, TN) + dot(al[...], w, TN)
    at = pl.multiple_of(core * 64, 64)
    o_ref[pl.ds(at, T)] = y_ref[pl.ds(at, T)] - v
    w0, w1 = w[:, :k_half], w[:, k_half:]
    u = (dot(gh[...], w0, TN) + dot(gl[...], w0, TN))[:64] + (dot(gh[...], w1, TN) + dot(gl[...], w1, TN))[64:]
    at = pl.multiple_of((1 - core) * T, 64)
    o_ref[pl.ds(at, 64)] = y_ref[pl.ds(at, 64)] - u


def sigma_diag(pos, e, y, w):
    m, order = y.shape
    k_all = w.shape[1]
    smem = pl.BlockSpec(memory_space=pltpu.SMEM)
    vm = pl.BlockSpec(memory_space=pltpu.VMEM)
    return pl.pallas_call(
        diag_kernel,
        out_shape=jax.ShapeDtypeStruct((m, order), F32),
        in_specs=[smem, vm, vm, vm],
        out_specs=vm,
        scratch_shapes=[
            pltpu.VMEM((k_all, T), BF16),
            pltpu.VMEM((k_all, T), BF16),
            pltpu.VMEM((k_all // 2, T), BF16),
            pltpu.VMEM((k_all // 2, T), BF16),
        ],
        name="sigma_diag",
    )(pos, e, y, w)


def ring(v, axis, step, n):
    return lax.ppermute(v, axis, [(i, (i + step) % n) for i in range(n)])


def spread(v, axis, n):
    return lax.all_to_all(jnp.broadcast_to(v[None], (n,) + v.shape), axis, 0, 0)


def local(parent_sigma, owner, ancestors, lfactors, panels):
    anc = ancestors[0]
    slots = owner[anc]
    x, core = lax.axis_index("x"), lax.axis_index("core")
    pos = jnp.stack([x, core]).astype(jnp.int32)
    at = (2 * x + core).astype(jnp.int32).reshape(1)

    pt = panels.T
    h = pt.shape[0] // 2
    right, left = ring(pt, "x", 1, 4), ring(pt, "x", -1, 4)

    rows_a, rows_b = code_rows(parent_sigma[0])
    got_b = spread(rows_b, "y", 4)
    got_a = spread(rows_a, "z", 8)
    lists_y = spread(ancestors, "y", 4).reshape(4, -1)
    lists_z = spread(ancestors, "z", 8).reshape(8, -1)
    sent_b = lax.all_to_all(pick(lists_z, got_b), "z", 0, 0)
    sent_a = lax.all_to_all(pick(lists_y, got_a), "y", 0, 0)

    right2, left2 = ring(right[:h], "x", 1, 4), ring(left[h:], "x", -1, 4)
    mine = [pt, right, left, right2, left2]
    other = [ring(v, "core", 1, 2) for v in mine]

    dh, dl = invert(lfactors)
    half = forward(at, lfactors, dh, dl, pt.shape[0])
    diag_inv = backward(half, lfactors, dh, dl)

    anc_rows, coded, whole = sigma_anc(slots, anc, pos, sent_a, sent_b, mine + other)
    coded = lax.all_to_all(coded, ("x", "core"), 0, 0)
    out = sigma_diag(pos, coded, diag_inv, whole)
    tiles = anc.shape[0]
    return anc_rows.reshape(1, tiles, -1, anc_rows.shape[1]), out.T


def solution(mesh):
    grid = Mesh(mesh.devices.reshape(4, 8, 4, 2), ("y", "z", "x", "core"))
    node, col = ("y", "z"), ("x", "core")
    return jax.shard_map(
        local,
        mesh=grid,
        in_specs=(P(node, col, None, None), P(), P(node, None), P(node, None), P(node, col)),
        out_specs=(P(node, None, col, None), P(node, col)),
        check_vma=False,
    )
```

```python
import jax
import jax.numpy as jnp
from jax import lax
from jax.experimental import pallas as pl
from jax.experimental.pallas import tpu as pltpu
from jax.sharding import Mesh, PartitionSpec as P


F32, BF16, I16 = jnp.float32, jnp.bfloat16, jnp.int16
T = 128
TOP = 32767.0
HBM = pl.BlockSpec(memory_space=pltpu.HBM)
SMEM = pl.BlockSpec(memory_space=pltpu.SMEM)
VMEM = pl.BlockSpec(memory_space=pltpu.VMEM)
NT = (((1,), (1,)), ((), ()))
NN = (((1,), (0,)), ((), ()))


def dot(a, b, dims=NN):
    return lax.dot_general(a, b, dims, preferred_element_type=F32)


def split(v):
    hi = v.astype(BF16)
    return hi, (v - hi.astype(F32)).astype(BF16)


def dot3(a, b, dims=NN):
    ah, al = a
    bh, bl = b
    return dot(ah, bh, dims) + (dot(ah, bl, dims) + dot(al, bh, dims))


def code_of(top):
    return jnp.clip(jnp.ceil(jnp.log2(top) * 256.0), -32000.0, 32000.0)


def scale_of(code):
    return jnp.exp2(code * (1.0 / 256.0))


def to_code(v):
    return jnp.clip(jnp.round(v), -TOP, TOP).astype(jnp.int32).astype(I16)


def encode(v, code):
    return to_code(v * (TOP / scale_of(code)))


def widen(q):
    return q.astype(jnp.int32).astype(F32)


LIST_LANE = 64


def code_rows_kernel(anc_ref, x_ref, a_ref, b_ref):
    rows, tiles = x_ref.shape[0], x_ref.shape[1]
    half = rows // 2
    lane = lax.broadcasted_iota(jnp.int32, (rows, T), 1)
    acc = jnp.zeros((rows, T), F32)
    for j in range(anc_ref.shape[0]):
        acc = jnp.where(lane == LIST_LANE + j, anc_ref[j].astype(F32), acc)
    for t in range(tiles + 1):
        if t < tiles:
            v = x_ref[:, t, :]
            code = code_of(jnp.max(jnp.abs(v), axis=1, keepdims=True))
            q = encode(v, code)
            acc = jnp.where(lane == t, code, acc)
        else:
            q = acc.astype(jnp.int32).astype(I16)
        for d in range(a_ref.shape[0]):
            a_ref[d, t] = q[:half]
        b_ref[t] = q[half:]


def code_rows(anc, x):
    rows, tiles, _ = x.shape
    shape = (tiles + 1, rows // 2, T)
    return pl.pallas_call(
        code_rows_kernel,
        out_shape=(jax.ShapeDtypeStruct((8,) + shape, I16), jax.ShapeDtypeStruct(shape, I16)),
        in_specs=[SMEM, VMEM],
        name="code_rows",
    )(anc, x)


def read_lists(sources, lv, ls, sem):
    for k, r in enumerate(sources):
        lv[k:k + 1] = widen(r[r.shape[0] - 1])[:1].astype(jnp.int32)
    copy = pltpu.make_async_copy(lv, ls, sem)
    copy.start()
    copy.wait()


def pick_z_kernel(a_ref, *refs):
    near, (o_ref, lv, ls, sem) = refs[:4], refs[4:]
    picks, tiles = o_ref.shape[2] - 1, near[0].shape[0] - 1
    read_lists([a_ref.at[k] for k in range(8)], lv, ls, sem)
    for d in range(8):
        for j in range(picks + 1):
            at = ls[d, LIST_LANE + j] if j < picks else tiles
            for k in range(4):
                o_ref[d, k, j] = near[k][at]


def pick_y_kernel(a_ref, *refs):
    near, o_refs, (lv, ls, sem) = refs[:4], refs[4:8], refs[8:]
    picks, tiles = o_refs[0].shape[1] - 1, near[0].shape[0] - 1
    read_lists(near, lv, ls, sem)
    for d in range(4):
        for j in range(picks + 1):
            at = ls[(4 - d) % 4, LIST_LANE + j] if j < picks else tiles
            o_refs[d][:, j] = a_ref[:, at]


LISTS = [pltpu.VMEM((8, T), jnp.int32), pltpu.SMEM((8, T), jnp.int32), pltpu.SemaphoreType.DMA(())]


def pick_z(far, near, picks):
    return pl.pallas_call(
        pick_z_kernel,
        out_shape=jax.ShapeDtypeStruct((8, 4, picks + 1) + near[0].shape[1:], I16),
        in_specs=[VMEM] * 5,
        scratch_shapes=LISTS,
        name="pick_z",
    )(far, *near)


def pick_y(far, near, picks):
    return pl.pallas_call(
        pick_y_kernel,
        out_shape=(jax.ShapeDtypeStruct((8, picks + 1) + near[0].shape[1:], I16),) * 4,
        in_specs=[VMEM] * 5,
        scratch_shapes=LISTS,
        name="pick_y",
    )(far, *near)


BLK = 256


def invert_blocks(l_ref, first, diag, sem, hi_ref, lo_ref, work=None):
    n = diag.shape[0]
    looped = work is not None
    copies = []
    for k in range(n):
        at = pl.ds((first + k) * BLK, BLK)
        copies.append(pltpu.make_async_copy(l_ref.at[at, at], diag.at[k], sem.at[k]))
        copies[k].start()
    row = lax.broadcasted_iota(jnp.int32, (BLK, BLK), 0)
    col = lax.broadcasted_iota(jnp.int32, (BLK, BLK), 1)
    eye = row == col
    blocks, invs = [], []
    for k in range(n):
        copies[k].wait()
        b = diag[k]
        f = b.astype(F32)
        d = jnp.where(eye, f, 0.0)
        rd = 1.0 / jnp.sum(d, axis=1, keepdims=True)
        cd = 1.0 / jnp.sum(d, axis=0, keepdims=True)
        pair = ((row >> 1) == (col >> 1)) & (row > col)
        invs.append(jnp.where(eye, rd, 0.0) - jnp.where(pair, f * rd * cd, 0.0))
        blocks.append(b)

    def level(s, invs):
        mask = ((row >> (s + 1)) == (col >> (s + 1))) & (((row >> s) & 1) > ((col >> s) & 1))
        out = []
        for k in range(n):
            c = jnp.where(mask, (diag[k] if looped else blocks[k]).astype(F32), 0.0).astype(BF16)
            ih, il = split(invs[k])
            t = split(dot(c, ih) + dot(c, il))
            out.append(invs[k] - dot3((ih, il), t))
        return out

    levels = BLK.bit_length() - 1
    if looped:
        def body(s, carry):
            for k, v in enumerate(level(s, [work[k] for k in range(n)])):
                work[k] = v
            return carry

        for k in range(n):
            work[k] = invs[k]
        lax.fori_loop(1, levels, body, 0)
        invs = [work[k] for k in range(n)]
    else:
        for s in range(1, levels):
            invs = level(s, invs)
    for k in range(n):
        hi_ref[k], lo_ref[k] = split(invs[k])


def invert_kernel(l_ref, hi_ref, lo_ref, diag, sem, work):
    invert_blocks(l_ref, 0, diag, sem, hi_ref, lo_ref, work)


def invert(lf, n):
    shape = jax.ShapeDtypeStruct((n, BLK, BLK), BF16)
    return pl.pallas_call(
        invert_kernel,
        out_shape=(shape, shape),
        in_specs=[HBM],
        out_specs=(VMEM,) * 2,
        scratch_shapes=[pltpu.VMEM((n, BLK, BLK), BF16), pltpu.SemaphoreType.DMA((n,)), pltpu.VMEM((n, BLK, BLK), F32)],
        name="invert",
    )(lf)


def forward_kernel(at_ref, l_ref, h0_ref, l0_ref, x_ref, hi_ref, lo_ref, xh, xl, lv, diag, sem):
    m = x_ref.shape[0]
    n = l_ref.shape[0] // BLK
    given = h0_ref.shape[0]
    panels = []
    for k in range(1, n):
        part = (pl.ds(k * BLK, BLK), pl.ds(0, k * BLK))
        panels.append(pltpu.make_async_copy(l_ref.at[part], lv.at[part], sem.at[n + k]))
        panels[k - 1].start()
    invert_blocks(l_ref, given, diag, sem, hi_ref, lo_ref)
    base = at_ref[0] * m
    row = lax.broadcasted_iota(jnp.int32, (m, BLK), 0) + base
    col = lax.broadcasted_iota(jnp.int32, (m, BLK), 1)
    for k in range(n):
        s = slice(k * BLK, (k + 1) * BLK)
        r = jnp.where(row == col + k * BLK, 1.0, 0.0)
        if k:
            panels[k - 1].wait()
            lk = lv[s, :k * BLK]
            r = r - (dot(xh[:, :k * BLK], lk, NT) + dot(xl[:, :k * BLK], lk, NT))
        inv = (h0_ref[k], l0_ref[k]) if k < given else (hi_ref[k - given], lo_ref[k - given])
        v = dot3(split(r), inv, NT)
        x_ref[:, s] = v
        xh[:, s], xl[:, s] = split(v)


def forward(at, lf, first, m):
    order = lf.shape[0]
    n = order // BLK
    left = n - first[0].shape[0]
    shape = jax.ShapeDtypeStruct((left, BLK, BLK), BF16)
    return pl.pallas_call(
        forward_kernel,
        out_shape=(jax.ShapeDtypeStruct((m, order), F32), shape, shape),
        in_specs=[SMEM, HBM, VMEM, VMEM],
        out_specs=(VMEM,) * 3,
        scratch_shapes=[
            pltpu.VMEM((m, order), BF16),
            pltpu.VMEM((m, order), BF16),
            pltpu.VMEM((order, order), BF16),
            pltpu.VMEM((left, BLK, BLK), BF16),
            pltpu.SemaphoreType.DMA((2 * n,)),
        ],
        name="forward",
    )(at, lf, *first)


def backward_kernel(x_ref, l_ref, h0_ref, l0_ref, h1_ref, l1_ref, y_ref, yh, yl, lv, sem):
    n = l_ref.shape[0] // BLK
    given = h0_ref.shape[0]
    copies = {}
    for k in reversed(range(n - 1)):
        part = (pl.ds((k + 1) * BLK, (n - 1 - k) * BLK), pl.ds(k * BLK, BLK))
        copies[k] = pltpu.make_async_copy(l_ref.at[part], lv.at[part], sem.at[k])
        copies[k].start()
    for k in reversed(range(n)):
        s = slice(k * BLK, (k + 1) * BLK)
        r = x_ref[:, s]
        if k < n - 1:
            e = (k + 1) * BLK
            copies[k].wait()
            lk = lv[e:, s]
            r = r - (dot(yh[:, e:], lk) + dot(yl[:, e:], lk))
        inv = (h0_ref[k], l0_ref[k]) if k < given else (h1_ref[k - given], l1_ref[k - given])
        v = dot3(split(r), inv)
        y_ref[:, s] = v
        yh[:, s], yl[:, s] = split(v)


def backward(x, lf, *invs):
    m, order = x.shape
    return pl.pallas_call(
        backward_kernel,
        out_shape=jax.ShapeDtypeStruct((m, order), F32),
        in_specs=[VMEM, HBM] + [VMEM] * 4,
        out_specs=VMEM,
        scratch_shapes=[
            pltpu.VMEM((m, order), BF16),
            pltpu.VMEM((m, order), BF16),
            pltpu.VMEM((order, order), BF16),
            pltpu.SemaphoreType.DMA((order // BLK,)),
        ],
        name="backward",
    )(x, lf, *invs)


def load_panels(core, blocks, pt, sem):
    m = blocks[0].shape[0]
    copies = []
    for k, role in enumerate((0, 1, 2, 3, 0, 2, 1, 3)):
        at = pl.multiple_of((core if k < 4 else 1 - core) * m, 64)
        copies.append(pltpu.make_async_copy(blocks[k], pt.at[role, pl.ds(at, m)], sem.at[k]))
    pairs = [(copies[0], copies[4]), (copies[1], copies[6]), (copies[2], copies[5]), (copies[3], copies[7])]
    for pair in pairs:
        for c in pair:
            c.start()
    return pairs


def chip_of(role, x, core):
    return (x + (0, 3 - 2 * core, 1 + 2 * core, 2)[role]) % 4


def anc_kernel(x_ref, core_ref, y_ref, own_ref, anc_ref, b_hbm, *refs):
    near, blocks, e_refs, (o_hbm, st, xv, b_ref, pt, ov, ev, sem) = refs[:4], refs[4:12], refs[13:21], refs[12:13] + refs[21:]
    n_anc = anc_ref.shape[0]
    n = n_anc * 16
    x, core, y = x_ref[0], core_ref[0], y_ref[0]
    copies = [pltpu.make_async_copy(near[k], xv.at[k], sem.at[8 + k]) for k in range(4)]
    copies.append(pltpu.make_async_copy(b_hbm, b_ref, sem.at[12]))
    for c in copies:
        c.start()
    panels = load_panels(core, blocks, pt, sem)
    for c in copies:
        c.wait()
    at = []
    for i in range(n_anc):
        s = own_ref[anc_ref[i]]
        at.append(((y - s // 8 + 4) % 4, s % 8))
    pick = [jnp.full((16, T), anc_ref[j], jnp.int32) for j in range(n_anc)]

    def rows(i, j):
        k, z = at[i]
        return jnp.concatenate([widen(xv[k, z, j]), widen(b_ref[z, k, j])], 0)

    scales = [scale_of(rows(i, n_anc)) * (-1.0 / TOP) for i in range(n_anc)]
    step = 4
    m = pt.shape[1]
    first = None
    for j0 in range(0, n_anc, step):
        for j in range(j0, j0 + step):
            for i in range(n_anc):
                wide = jnp.take_along_axis(scales[i], pick[j], axis=1)
                hi, lo = split(rows(i, j) * wide)
                st[i * 16:(i + 1) * 16, j * T:(j + 1) * T] = hi
                st[n + i * 16:n + (i + 1) * 16, j * T:(j + 1) * T] = lo
        if j0 == 0:
            for c in panels[0]:
                c.wait()
        ks = slice(j0 * T, (j0 + step) * T)
        v = dot(st[:, ks], pt[0, :, ks], NT)
        first = v if first is None else first + v
    lane = lax.broadcasted_iota(jnp.int32, (n, T), 1)
    sub = lax.broadcasted_iota(jnp.int32, (n, T), 0) % 16 + (2 * x + core) * 16
    here = lane == sub
    low = lane < 64
    ends = []
    v = first
    for role in range(4):
        ahead = None
        if role < 3:
            for c in panels[role + 1]:
                c.wait()
            ahead = dot(st[...], pt[role + 1], NT)
        v = v[:n] + v[n:]
        g = chip_of(role, x, core)
        cols = pl.ds(pl.multiple_of(g * m, T), m)
        ov[:, cols] = v
        mid = v[:, T:2 * T]
        for side in range(2):
            whole = v[:, :T] if side == 0 else v[:, 2 * T:]
            rest = jnp.where(low if side == 0 else ~low, mid, 0.0)
            code = code_of(jnp.max(jnp.maximum(jnp.abs(whole), jnp.abs(rest)), axis=1, keepdims=True))
            inv = TOP / scale_of(code)
            e = ev.at[2 * role + side]
            e[:n] = to_code(whole * inv)
            p = rest * inv
            top, bottom = p[:n // 2], p[n // 2:]
            both = top + pltpu.roll(bottom, 64, 1) if side == 0 else pltpu.roll(top, 64, 1) + bottom
            e[n:n + n // 2] = to_code(both)
            grid = jnp.sum(jnp.where(here, code, 0.0).reshape(n_anc, 16, T), axis=1)
            e[n + n // 2:] = grid.astype(jnp.int32).astype(I16)
        ends.append(pltpu.make_async_copy(ov.at[:, cols], o_hbm.at[:, cols], sem.at[role]))
        ends[-1].start()
        for far in range(2):
            k = 2 * role + far
            ends.append(pltpu.make_async_copy(ev.at[2 * role + (core + far) % 2], e_refs[k], sem.at[4 + k]))
            ends[-1].start()
        v = ahead
    for c in ends:
        c.wait()


def sigma_anc(place, owner, anc, near, b, blocks):
    n_anc = anc.shape[0]
    m, k_all = blocks[0].shape
    order = 8 * m
    coded = (n_anc * 25, T)
    return pl.pallas_call(
        anc_kernel,
        out_shape=(jax.ShapeDtypeStruct((n_anc * 16, order), F32),) + (jax.ShapeDtypeStruct(coded, I16),) * 8,
        in_specs=[SMEM] * 5 + [HBM] * 13,
        out_specs=(HBM,) * 9,
        scratch_shapes=[
            pltpu.VMEM((n_anc * 32, k_all), BF16),
            pltpu.VMEM((4,) + near[0].shape, I16),
            pltpu.VMEM(b.shape, I16),
            pltpu.VMEM((4, 2 * m, k_all), BF16),
            pltpu.VMEM((n_anc * 16, order), F32),
            pltpu.VMEM((8,) + coded, I16),
            pltpu.SemaphoreType.DMA((13,)),
        ],
        name="sigma_anc",
    )(*place, owner, anc, b, *near, *blocks)


def diag_kernel(x_ref, core_ref, y_hbm, *refs):
    e_refs, blocks, (o_hbm, o_ref, y_ref, e_ref, xt, sc, pt, sem) = refs[:8], refs[8:16], refs[16:]
    n_anc = e_ref.shape[1] // 25
    n = n_anc * 16
    half = n_anc // 2
    x, core = x_ref[0], core_ref[0]
    copies = []
    for k in range(8):
        c = core if k % 2 == 0 else 1 - core
        at = 2 * ((x + (0, 1 + 2 * c, 3 - 2 * c, 2)[k // 2]) % 4) + c
        copies.append(pltpu.make_async_copy(e_refs[k], e_ref.at[at], sem.at[8 + k]))
        copies[k].start()
    panels = load_panels(core, blocks, pt, sem)
    base = pltpu.make_async_copy(y_hbm, y_ref, sem.at[16])
    base.start()
    for c in copies:
        c.wait()
    codes = jnp.zeros((n_anc, T), F32)
    for c in range(8):
        codes = codes + widen(e_ref[c, n + n // 2:])
    sc[...] = scale_of(codes) * (1.0 / TOP)

    def rows(at):
        return jnp.concatenate([widen(e_ref[c, at:at + 16]) for c in range(8)], 0).T

    for i in range(half):
        g = rows(n + i * 16)
        for k in range(2):
            j = i + k * half
            at = slice(j * T, (j + 1) * T)
            s = sc[j:j + 1]
            xt[0:T, at], xt[T:2 * T, at] = split(rows(j * 16) * s)
            xt[2 * T:2 * T + 64, at], xt[2 * T + 64:, at] = split(g[k * 64:(k + 1) * 64] * s)

    m = pt.shape[1]
    ends = []
    v = None
    for role in range(-1, 4):
        ahead = None
        if role < 3:
            for c in panels[role + 1]:
                c.wait()
            ahead = dot(xt[...], pt[role + 1], NT)
        if role < 0:
            base.wait()
        else:
            at = pl.ds(pl.multiple_of(chip_of(role, x, core) * m, T), m)
            r = pl.ds(pl.multiple_of(core * 64, 64), T)
            o_ref[r, at] = y_ref[r, at] - (v[:T] + v[T:2 * T])
            r = pl.ds(pl.multiple_of((1 - core) * T, 64), 64)
            o_ref[r, at] = y_ref[r, at] - (v[2 * T:2 * T + 64] + v[2 * T + 64:])
            ends.append(pltpu.make_async_copy(o_ref.at[:, at], o_hbm.at[:, at], sem.at[role]))
            ends[-1].start()
        v = ahead
    for c in ends:
        c.wait()


def sigma_diag(place, e, y, blocks):
    m, order = y.shape
    k_all = blocks[0].shape[1]
    return pl.pallas_call(
        diag_kernel,
        out_shape=jax.ShapeDtypeStruct((m, order), F32),
        in_specs=[SMEM] * 2 + [HBM] * 17,
        out_specs=HBM,
        scratch_shapes=[
            pltpu.VMEM((m, order), F32),
            pltpu.VMEM((m, order), F32),
            pltpu.VMEM((8,) + e[0].shape, I16),
            pltpu.VMEM((2 * m, k_all), BF16),
            pltpu.VMEM((e[0].shape[0] // 25, T), F32),
            pltpu.VMEM((4, 2 * m, k_all), BF16),
            pltpu.SemaphoreType.DMA((17,)),
        ],
        name="sigma_diag",
    )(*place[:2], y, *e, *blocks)


def ring(v, axis, step, n):
    return lax.ppermute(v, axis, [(i, (i + step) % n) for i in range(n)])


def swap(v, axis):
    return lax.all_to_all(v, axis, 0, 0)


def steps(parent_sigma, owner, ancestors, lfactors, panels):
    anc = ancestors[0]
    n_anc = anc.shape[0]
    place = [lax.axis_index(name).astype(jnp.int32).reshape(1) for name in ("x", "core", "y")]
    at = 2 * place[0] + place[1]

    rows_a, rows_b = code_rows(anc, parent_sigma[0])
    far = swap(rows_a, "z")
    near = [rows_b] + [ring(rows_b, "y", k, 4) for k in (1, 2, 3)]
    pt = panels.T
    lane = ("x", "core")
    out_way = [(2 * i + c, 2 * ((i + 1 - 2 * c) % 4) + c) for i in range(4) for c in range(2)]
    back_way = [(q, p) for p, q in out_way]
    cross_way = [(p, q + 1 - 2 * (q % 2)) for p, q in out_way]
    mine = [pt, lax.ppermute(pt, lane, out_way), lax.ppermute(pt, lane, back_way)]
    other = [ring(v, "core", 1, 2) for v in mine]
    mine.append(lax.ppermute(mine[1], lane, out_way))
    other.append(lax.ppermute(mine[1], lane, cross_way))

    first = invert(lfactors, lfactors.shape[0] // BLK // 2)
    sent_b = swap(pick_z(far, near, n_anc), "z")
    picked = pick_y(far, near, n_anc)
    sent_a = [picked[0]] + [ring(picked[k], "y", k, 4) for k in (1, 2, 3)]

    half, *second = forward(at, lfactors, first, pt.shape[0])
    diag_inv = backward(half, lfactors, *first, *second)
    rows, *coded = sigma_anc(place, owner, anc, sent_a, sent_b, mine + other)
    for k in range(1, 8):
        step = ((0, 0), (3, 1), (1, 3), (2, 2))[k // 2]
        pairs = [(2 * i + c, 2 * ((i + step[c]) % 4) + (c + k) % 2) for i in range(4) for c in range(2)]
        coded[k] = lax.ppermute(coded[k], lane, pairs)
    out = sigma_diag(place, coded, diag_inv, mine + other)
    return rows.reshape(1, n_anc, -1, rows.shape[-1]), out.T


def solution(mesh):
    grid = Mesh(mesh.devices.reshape(4, 8, 4, 2), ("y", "z", "x", "core"))
    node, col = ("y", "z"), ("x", "core")
    return jax.shard_map(
        steps,
        mesh=grid,
        in_specs=(P(node, col, None, None), P(), P(node, None), P(node, None), P(node, col)),
        out_specs=(P(node, None, col, None), P(node, col)),
        check_vma=False,
    )
```

```python
import jax
import jax.numpy as jnp
from jax import lax
from jax.experimental import pallas as pl
from jax.experimental.pallas import tpu as pltpu
from jax.sharding import Mesh, PartitionSpec as P


F32, BF16, I16 = jnp.float32, jnp.bfloat16, jnp.int16
T = 128
TOP = 32767.0
HBM = pl.BlockSpec(memory_space=pltpu.HBM)
SMEM = pl.BlockSpec(memory_space=pltpu.SMEM)
VMEM = pl.BlockSpec(memory_space=pltpu.VMEM)
NT = (((1,), (1,)), ((), ()))
NN = (((1,), (0,)), ((), ()))


def dot(a, b, dims=NN):
    return lax.dot_general(a, b, dims, preferred_element_type=F32)


def split(v):
    hi = v.astype(BF16)
    return hi, (v - hi.astype(F32)).astype(BF16)


def dot3(a, b, dims=NN):
    ah, al = a
    bh, bl = b
    return dot(ah, bh, dims) + (dot(ah, bl, dims) + dot(al, bh, dims))


def code_of(top):
    return jnp.clip(jnp.ceil(jnp.log2(top) * 256.0), -32000.0, 32000.0)


def scale_of(code):
    return jnp.exp2(code * (1.0 / 256.0))


def to_code(v):
    return jnp.clip(jnp.round(v), -TOP, TOP).astype(jnp.int32).astype(I16)


def encode(v, code):
    return to_code(v * (TOP / scale_of(code)))


def widen(q):
    return q.astype(jnp.int32).astype(F32)


LIST_LANE = 64


def code_rows_kernel(anc_ref, x_ref, a_ref, b_ref):
    rows, tiles = x_ref.shape[0], x_ref.shape[1]
    half = rows // 2
    lane = lax.broadcasted_iota(jnp.int32, (rows, T), 1)
    acc = jnp.zeros((rows, T), F32)
    for j in range(anc_ref.shape[0]):
        acc = jnp.where(lane == LIST_LANE + j, anc_ref[j].astype(F32), acc)
    for t in range(tiles + 1):
        if t < tiles:
            v = x_ref[:, t, :]
            code = code_of(jnp.max(jnp.abs(v), axis=1, keepdims=True))
            q = encode(v, code)
            acc = jnp.where(lane == t, code, acc)
        else:
            q = acc.astype(jnp.int32).astype(I16)
        for d in range(a_ref.shape[0]):
            a_ref[d, t] = q[:half]
        b_ref[t] = q[half:]


def code_rows(anc, x):
    rows, tiles, _ = x.shape
    shape = (tiles + 1, rows // 2, T)
    return pl.pallas_call(
        code_rows_kernel,
        out_shape=(jax.ShapeDtypeStruct((8,) + shape, I16), jax.ShapeDtypeStruct(shape, I16)),
        in_specs=[SMEM, VMEM],
        name="code_rows",
    )(anc, x)


def read_lists(sources, lv, ls, sem):
    for k, r in enumerate(sources):
        lv[k:k + 1] = widen(r[r.shape[0] - 1])[:1].astype(jnp.int32)
    copy = pltpu.make_async_copy(lv, ls, sem)
    copy.start()
    copy.wait()


def pick_z_kernel(a_ref, *refs):
    near, (o_ref, lv, ls, sem) = refs[:4], refs[4:]
    picks, tiles = o_ref.shape[2] - 1, near[0].shape[0] - 1
    read_lists([a_ref.at[k] for k in range(8)], lv, ls, sem)
    for d in range(8):
        for j in range(picks + 1):
            at = ls[d, LIST_LANE + j] if j < picks else tiles
            for k in range(4):
                o_ref[d, k, j] = near[k][at]


def pick_y_kernel(a_ref, *refs):
    near, o_refs, (lv, ls, sem) = refs[:4], refs[4:8], refs[8:]
    picks, tiles = o_refs[0].shape[1] - 1, near[0].shape[0] - 1
    read_lists(near, lv, ls, sem)
    for d in range(4):
        for j in range(picks + 1):
            at = ls[(4 - d) % 4, LIST_LANE + j] if j < picks else tiles
            o_refs[d][:, j] = a_ref[:, at]


LISTS = [pltpu.VMEM((8, T), jnp.int32), pltpu.SMEM((8, T), jnp.int32), pltpu.SemaphoreType.DMA(())]


def pick_z(far, near, picks):
    return pl.pallas_call(
        pick_z_kernel,
        out_shape=jax.ShapeDtypeStruct((8, 4, picks + 1) + near[0].shape[1:], I16),
        in_specs=[VMEM] * 5,
        scratch_shapes=LISTS,
        name="pick_z",
    )(far, *near)


def pick_y(far, near, picks):
    return pl.pallas_call(
        pick_y_kernel,
        out_shape=(jax.ShapeDtypeStruct((8, picks + 1) + near[0].shape[1:], I16),) * 4,
        in_specs=[VMEM] * 5,
        scratch_shapes=LISTS,
        name="pick_y",
    )(far, *near)


BLK = 256


def invert_blocks(l_ref, first, diag, sem, hi_ref, lo_ref, work=None):
    n = diag.shape[0]
    looped = work is not None
    copies = []
    for k in range(n):
        at = pl.ds((first + k) * BLK, BLK)
        copies.append(pltpu.make_async_copy(l_ref.at[at, at], diag.at[k], sem.at[k]))
        copies[k].start()
    row = lax.broadcasted_iota(jnp.int32, (BLK, BLK), 0)
    col = lax.broadcasted_iota(jnp.int32, (BLK, BLK), 1)
    eye = row == col
    blocks, invs = [], []
    for k in range(n):
        copies[k].wait()
        b = diag[k]
        f = b.astype(F32)
        d = jnp.where(eye, f, 0.0)
        rd = 1.0 / jnp.sum(d, axis=1, keepdims=True)
        cd = 1.0 / jnp.sum(d, axis=0, keepdims=True)
        pair = ((row >> 1) == (col >> 1)) & (row > col)
        invs.append(jnp.where(eye, rd, 0.0) - jnp.where(pair, f * rd * cd, 0.0))
        blocks.append(b)

    def level(s, invs):
        mask = ((row >> (s + 1)) == (col >> (s + 1))) & (((row >> s) & 1) > ((col >> s) & 1))
        out = []
        for k in range(n):
            c = jnp.where(mask, (diag[k] if looped else blocks[k]).astype(F32), 0.0).astype(BF16)
            ih, il = split(invs[k])
            t = split(dot(c, ih) + dot(c, il))
            out.append(invs[k] - dot3((ih, il), t))
        return out

    levels = BLK.bit_length() - 1
    if looped:
        def body(s, carry):
            for k, v in enumerate(level(s, [work[k] for k in range(n)])):
                work[k] = v
            return carry

        for k in range(n):
            work[k] = invs[k]
        lax.fori_loop(1, levels, body, 0)
        invs = [work[k] for k in range(n)]
    else:
        for s in range(1, levels):
            invs = level(s, invs)
    for k in range(n):
        hi_ref[k], lo_ref[k] = split(invs[k])


def invert_kernel(l_ref, hi_ref, lo_ref, diag, sem, work):
    invert_blocks(l_ref, 0, diag, sem, hi_ref, lo_ref, work)


def invert(lf, n):
    shape = jax.ShapeDtypeStruct((n, BLK, BLK), BF16)
    return pl.pallas_call(
        invert_kernel,
        out_shape=(shape, shape),
        in_specs=[HBM],
        out_specs=(VMEM,) * 2,
        scratch_shapes=[pltpu.VMEM((n, BLK, BLK), BF16), pltpu.SemaphoreType.DMA((n,)), pltpu.VMEM((n, BLK, BLK), F32)],
        name="invert",
    )(lf)


def forward_kernel(at_ref, l_ref, h0_ref, l0_ref, x_ref, hi_ref, lo_ref, xh, xl, lv, diag, sem):
    m = x_ref.shape[0]
    n = l_ref.shape[0] // BLK
    given = h0_ref.shape[0]
    panels = []
    for k in range(1, n):
        part = (pl.ds(k * BLK, BLK), pl.ds(0, k * BLK))
        panels.append(pltpu.make_async_copy(l_ref.at[part], lv.at[part], sem.at[n + k]))
        panels[k - 1].start()
    invert_blocks(l_ref, given, diag, sem, hi_ref, lo_ref)
    base = at_ref[0] * m
    row = lax.broadcasted_iota(jnp.int32, (m, BLK), 0) + base
    col = lax.broadcasted_iota(jnp.int32, (m, BLK), 1)
    for k in range(n):
        s = slice(k * BLK, (k + 1) * BLK)
        r = jnp.where(row == col + k * BLK, 1.0, 0.0)
        if k:
            panels[k - 1].wait()
            lk = lv[s, :k * BLK]
            r = r - (dot(xh[:, :k * BLK], lk, NT) + dot(xl[:, :k * BLK], lk, NT))
        inv = (h0_ref[k], l0_ref[k]) if k < given else (hi_ref[k - given], lo_ref[k - given])
        v = dot3(split(r), inv, NT)
        x_ref[:, s] = v
        xh[:, s], xl[:, s] = split(v)


def forward(at, lf, first, m):
    order = lf.shape[0]
    n = order // BLK
    left = n - first[0].shape[0]
    shape = jax.ShapeDtypeStruct((left, BLK, BLK), BF16)
    return pl.pallas_call(
        forward_kernel,
        out_shape=(jax.ShapeDtypeStruct((m, order), F32), shape, shape),
        in_specs=[SMEM, HBM, VMEM, VMEM],
        out_specs=(VMEM,) * 3,
        scratch_shapes=[
            pltpu.VMEM((m, order), BF16),
            pltpu.VMEM((m, order), BF16),
            pltpu.VMEM((order, order), BF16),
            pltpu.VMEM((left, BLK, BLK), BF16),
            pltpu.SemaphoreType.DMA((2 * n,)),
        ],
        name="forward",
    )(at, lf, *first)


def backward_kernel(x_ref, l_ref, h0_ref, l0_ref, h1_ref, l1_ref, y_ref, yh, yl, lv, sem):
    n = l_ref.shape[0] // BLK
    given = h0_ref.shape[0]
    copies = {}
    for k in reversed(range(n - 1)):
        part = (pl.ds((k + 1) * BLK, (n - 1 - k) * BLK), pl.ds(k * BLK, BLK))
        copies[k] = pltpu.make_async_copy(l_ref.at[part], lv.at[part], sem.at[k])
        copies[k].start()
    for k in reversed(range(n)):
        s = slice(k * BLK, (k + 1) * BLK)
        r = x_ref[:, s]
        if k < n - 1:
            e = (k + 1) * BLK
            copies[k].wait()
            lk = lv[e:, s]
            r = r - (dot(yh[:, e:], lk) + dot(yl[:, e:], lk))
        inv = (h0_ref[k], l0_ref[k]) if k < given else (h1_ref[k - given], l1_ref[k - given])
        v = dot3(split(r), inv)
        y_ref[:, s] = v
        yh[:, s], yl[:, s] = split(v)


def backward(x, lf, *invs):
    m, order = x.shape
    return pl.pallas_call(
        backward_kernel,
        out_shape=jax.ShapeDtypeStruct((m, order), F32),
        in_specs=[VMEM, HBM] + [VMEM] * 4,
        out_specs=VMEM,
        scratch_shapes=[
            pltpu.VMEM((m, order), BF16),
            pltpu.VMEM((m, order), BF16),
            pltpu.VMEM((order, order), BF16),
            pltpu.SemaphoreType.DMA((order // BLK,)),
        ],
        name="backward",
    )(x, lf, *invs)


def load_panels(core, blocks, pt, sem):
    m = blocks[0].shape[0]
    h = m // 2
    copies = []
    for k, role in enumerate((0, 1, 2, 3, 0, 2, 1, 3)):
        both = []
        for p in range(2):
            at = pl.multiple_of((core if k < 4 else 1 - core) * m + p * h, 32)
            src = blocks[k].at[pl.ds(p * h, h)]
            both.append(pltpu.make_async_copy(src, pt.at[role, pl.ds(at, h)], sem.at[2 * k + p]))
        copies.append(both)
    pairs = [copies[0] + copies[4], copies[1] + copies[6], copies[2] + copies[5], copies[3] + copies[7]]
    for pair in pairs:
        for c in pair:
            c.start()
    return pairs


def chip_of(role, x, core):
    return (x + (0, 3 - 2 * core, 1 + 2 * core, 2)[role]) % 4


def anc_kernel(x_ref, core_ref, y_ref, own_ref, anc_ref, b_hbm, *refs):
    near, blocks, e_refs, (o_hbm, st, xv, b_ref, pt, ov, ev, sem) = refs[:4], refs[4:12], refs[13:21], refs[12:13] + refs[21:]
    n_anc = anc_ref.shape[0]
    n = n_anc * 16
    x, core, y = x_ref[0], core_ref[0], y_ref[0]
    copies = [pltpu.make_async_copy(near[k], xv.at[k], sem.at[16 + k]) for k in range(4)]
    copies.append(pltpu.make_async_copy(b_hbm, b_ref, sem.at[20]))
    for c in copies:
        c.start()
    panels = load_panels(core, blocks, pt, sem)
    for c in copies:
        c.wait()
    at = []
    for i in range(n_anc):
        s = own_ref[anc_ref[i]]
        at.append(((y - s // 8 + 4) % 4, s % 8))
    pick = [jnp.full((16, T), anc_ref[j], jnp.int32) for j in range(n_anc)]

    def rows(i, j):
        k, z = at[i]
        return jnp.concatenate([widen(xv[k, z, j]), widen(b_ref[z, k, j])], 0)

    scales = [scale_of(rows(i, n_anc)) * (-1.0 / TOP) for i in range(n_anc)]
    step = 4
    m = pt.shape[1]
    first = None
    for j0 in range(0, n_anc, step):
        for j in range(j0, j0 + step):
            for i in range(n_anc):
                wide = jnp.take_along_axis(scales[i], pick[j], axis=1)
                hi, lo = split(rows(i, j) * wide)
                st[i * 16:(i + 1) * 16, j * T:(j + 1) * T] = hi
                st[n + i * 16:n + (i + 1) * 16, j * T:(j + 1) * T] = lo
        if j0 == 0:
            for c in panels[0]:
                c.wait()
        ks = slice(j0 * T, (j0 + step) * T)
        v = dot(st[:, ks], pt[0, :, ks], NT)
        first = v if first is None else first + v
    lane = lax.broadcasted_iota(jnp.int32, (n, T), 1)
    sub = lax.broadcasted_iota(jnp.int32, (n, T), 0) % 16 + (2 * x + core) * 16
    here = lane == sub
    low = lane < 64
    ends = []
    v = first
    for role in range(4):
        ahead = None
        if role < 3:
            for c in panels[role + 1]:
                c.wait()
            ahead = dot(st[...], pt[role + 1], NT)
        v = v[:n] + v[n:]
        g = chip_of(role, x, core)
        cols = pl.ds(pl.multiple_of(g * m, T), m)
        ov[:, cols] = v
        mid = v[:, T:2 * T]
        for side in range(2):
            whole = v[:, :T] if side == 0 else v[:, 2 * T:]
            rest = jnp.where(low if side == 0 else ~low, mid, 0.0)
            code = code_of(jnp.max(jnp.maximum(jnp.abs(whole), jnp.abs(rest)), axis=1, keepdims=True))
            inv = TOP / scale_of(code)
            e = ev.at[2 * role + side]
            e[:n] = to_code(whole * inv)
            p = rest * inv
            top, bottom = p[:n // 2], p[n // 2:]
            both = top + pltpu.roll(bottom, 64, 1) if side == 0 else pltpu.roll(top, 64, 1) + bottom
            e[n:n + n // 2] = to_code(both)
            grid = jnp.sum(jnp.where(here, code, 0.0).reshape(n_anc, 16, T), axis=1)
            e[n + n // 2:] = grid.astype(jnp.int32).astype(I16)
        ends.append(pltpu.make_async_copy(ov.at[:, cols], o_hbm.at[:, cols], sem.at[21 + role]))
        ends[-1].start()
        for far in range(2):
            k = 2 * role + far
            ends.append(pltpu.make_async_copy(ev.at[2 * role + (core + far) % 2], e_refs[k], sem.at[25 + k]))
            ends[-1].start()
        v = ahead
    for c in ends:
        c.wait()


def sigma_anc(place, owner, anc, near, b, blocks):
    n_anc = anc.shape[0]
    m, k_all = blocks[0].shape
    order = 8 * m
    coded = (n_anc * 25, T)
    return pl.pallas_call(
        anc_kernel,
        out_shape=(jax.ShapeDtypeStruct((n_anc * 16, order), F32),) + (jax.ShapeDtypeStruct(coded, I16),) * 8,
        in_specs=[SMEM] * 5 + [HBM] * 13,
        out_specs=(HBM,) * 9,
        scratch_shapes=[
            pltpu.VMEM((n_anc * 32, k_all), BF16),
            pltpu.VMEM((4,) + near[0].shape, I16),
            pltpu.VMEM(b.shape, I16),
            pltpu.VMEM((4, 2 * m, k_all), BF16),
            pltpu.VMEM((n_anc * 16, order), F32),
            pltpu.VMEM((8,) + coded, I16),
            pltpu.SemaphoreType.DMA((33,)),
        ],
        name="sigma_anc",
    )(*place, owner, anc, b, *near, *blocks)


def diag_kernel(x_ref, core_ref, y_hbm, *refs):
    e_refs, blocks, (o_hbm, o_ref, y_ref, e_ref, xt, sc, pt, sem) = refs[:8], refs[8:16], refs[16:]
    n_anc = e_ref.shape[1] // 25
    n = n_anc * 16
    half = n_anc // 2
    x, core = x_ref[0], core_ref[0]
    copies = []
    for k in range(8):
        c = core if k % 2 == 0 else 1 - core
        at = 2 * ((x + (0, 1 + 2 * c, 3 - 2 * c, 2)[k // 2]) % 4) + c
        copies.append(pltpu.make_async_copy(e_refs[k], e_ref.at[at], sem.at[16 + k]))
        copies[k].start()
    panels = load_panels(core, blocks, pt, sem)
    base = pltpu.make_async_copy(y_hbm, y_ref, sem.at[24])
    base.start()
    for c in copies:
        c.wait()
    codes = jnp.zeros((n_anc, T), F32)
    for c in range(8):
        codes = codes + widen(e_ref[c, n + n // 2:])
    sc[...] = scale_of(codes) * (1.0 / TOP)

    def rows(at):
        return jnp.concatenate([widen(e_ref[c, at:at + 16]) for c in range(8)], 0).T

    for i in range(half):
        g = rows(n + i * 16)
        for k in range(2):
            j = i + k * half
            at = slice(j * T, (j + 1) * T)
            s = sc[j:j + 1]
            xt[0:T, at], xt[T:2 * T, at] = split(rows(j * 16) * s)
            xt[2 * T:2 * T + 64, at], xt[2 * T + 64:, at] = split(g[k * 64:(k + 1) * 64] * s)

    m = pt.shape[1]
    ends = []
    v = None
    for role in range(-1, 4):
        ahead = None
        if role < 3:
            for c in panels[role + 1]:
                c.wait()
            ahead = dot(xt[...], pt[role + 1], NT)
        if role < 0:
            base.wait()
        else:
            at = pl.ds(pl.multiple_of(chip_of(role, x, core) * m, T), m)
            r = pl.ds(pl.multiple_of(core * 64, 64), T)
            o_ref[r, at] = y_ref[r, at] - (v[:T] + v[T:2 * T])
            r = pl.ds(pl.multiple_of((1 - core) * T, 64), 64)
            o_ref[r, at] = y_ref[r, at] - (v[2 * T:2 * T + 64] + v[2 * T + 64:])
            ends.append(pltpu.make_async_copy(o_ref.at[:, at], o_hbm.at[:, at], sem.at[25 + role]))
            ends[-1].start()
        v = ahead
    for c in ends:
        c.wait()


def sigma_diag(place, e, y, blocks):
    m, order = y.shape
    k_all = blocks[0].shape[1]
    return pl.pallas_call(
        diag_kernel,
        out_shape=jax.ShapeDtypeStruct((m, order), F32),
        in_specs=[SMEM] * 2 + [HBM] * 17,
        out_specs=HBM,
        scratch_shapes=[
            pltpu.VMEM((m, order), F32),
            pltpu.VMEM((m, order), F32),
            pltpu.VMEM((8,) + e[0].shape, I16),
            pltpu.VMEM((2 * m, k_all), BF16),
            pltpu.VMEM((e[0].shape[0] // 25, T), F32),
            pltpu.VMEM((4, 2 * m, k_all), BF16),
            pltpu.SemaphoreType.DMA((29,)),
        ],
        name="sigma_diag",
    )(*place[:2], y, *e, *blocks)


def ring(v, axis, step, n):
    return lax.ppermute(v, axis, [(i, (i + step) % n) for i in range(n)])


def swap(v, axis):
    return lax.all_to_all(v, axis, 0, 0)


def steps(parent_sigma, owner, ancestors, lfactors, panels):
    anc = ancestors[0]
    n_anc = anc.shape[0]
    place = [lax.axis_index(name).astype(jnp.int32).reshape(1) for name in ("x", "core", "y")]
    at = 2 * place[0] + place[1]

    rows_a, rows_b = code_rows(anc, parent_sigma[0])
    far = swap(rows_a, "z")
    near = [rows_b] + [ring(rows_b, "y", k, 4) for k in (1, 2, 3)]
    pt = panels.T
    lane = ("x", "core")
    out_way = [(2 * i + c, 2 * ((i + 1 - 2 * c) % 4) + c) for i in range(4) for c in range(2)]
    back_way = [(q, p) for p, q in out_way]
    cross_way = [(p, q + 1 - 2 * (q % 2)) for p, q in out_way]
    mine = [pt, lax.ppermute(pt, lane, out_way), lax.ppermute(pt, lane, back_way)]
    other = [ring(v, "core", 1, 2) for v in mine]
    mine.append(lax.ppermute(mine[1], lane, out_way))
    other.append(lax.ppermute(mine[1], lane, cross_way))

    first = invert(lfactors, lfactors.shape[0] // BLK // 2)
    sent_b = swap(pick_z(far, near, n_anc), "z")
    picked = pick_y(far, near, n_anc)
    sent_a = [picked[0]] + [ring(picked[k], "y", k, 4) for k in (1, 2, 3)]

    half, *second = forward(at, lfactors, first, pt.shape[0])
    diag_inv = backward(half, lfactors, *first, *second)
    rows, *coded = sigma_anc(place, owner, anc, sent_a, sent_b, mine + other)
    for k in range(1, 8):
        step = ((0, 0), (3, 1), (1, 3), (2, 2))[k // 2]
        pairs = [(2 * i + c, 2 * ((i + step[c]) % 4) + (c + k) % 2) for i in range(4) for c in range(2)]
        coded[k] = lax.ppermute(coded[k], lane, pairs)
    out = sigma_diag(place, coded, diag_inv, mine + other)
    return rows.reshape(1, n_anc, -1, rows.shape[-1]), out.T


def solution(mesh):
    grid = Mesh(mesh.devices.reshape(4, 8, 4, 2), ("y", "z", "x", "core"))
    node, col = ("y", "z"), ("x", "core")
    return jax.shard_map(
        steps,
        mesh=grid,
        in_specs=(P(node, col, None, None), P(), P(node, None), P(node, None), P(node, col)),
        out_specs=(P(node, None, col, None), P(node, col)),
        check_vma=False,
    )
```
